32 devices in a mesh: groups: 2 (over x), row: 16 (over z, y, core).
Axes of the slice: x: 2, y: 2, z: 4, core: 2. Of those that a mesh axis runs over, the one named last changes fastest.
Arguments:
- walkers: bfloat16 [512, 256, 64], P(('groups', 'row')), parts along dimension 0, may hold values from -6 to 6
- inv_intersection: bfloat16 [512, 64, 64], P(('groups', 'row')), parts along dimension 0, may hold values from -0.75 to 0.75
- copies: int32 [512], P(('groups', 'row')), parts along dimension 0, may hold values from 0 to 3, as said below
- deal: int32 [32], P('groups'), parts along dimension 0, may hold values from 0 to 15, each once
- trial: bfloat16 [512, 64], P('groups'), parts along dimension 0, may hold values from -6 to 6
- chol: bfloat16 [8192, 256, 256], P('groups', 'row'), parts along dimension 0, may hold values from -0.15625 to 0.15625
- noise: float32 [512, 4096], P(('groups', 'row')), parts along dimension 0, may hold values from -6 to 6
Outputs:
- propagated: bfloat16 [512, 256, 64], P(('groups', 'row')), parts along dimension 0
- force_bias: float32 [512, 4096], P(('groups', 'row')), parts along dimension 0
The draws below stay inside these ranges and needn't reach their ends.
There are 2 independent parts, one for each index of `groups`. The reference program is written for one: setup_inputs(seed, part) draws one part's arguments, and reference() takes and returns one part's arrays. A program takes and returns all parts, laid end to end along the dimension named above; each array names one. Nothing has to cross between parts.
Inputs may be any that keep to these rules, and one draw needn't show every extreme that they name: The copy counts sum to 256; the walkers of one device have at most 32 copies together, and some device reaches that.
All inputs are finite; a program needn't handle non-finite values.
Results may differ from the reference program's by a relative error of at most 0.023.
Values may be sent and summed in bfloat16 or wider, within the bound.
A program may use at most 128 MiB of HBM per device.

```python
import jax
import jax.numpy as jnp

ORBITALS = 256
ELECTRONS = 64
CHOL = 4096
W_DEV = 16
WALKERS = 256
N_ROW = 16


def draw_copies(key, part):
    base = jax.random.fold_in(key, 7)
    first_key, second_key, third_key = jax.random.split(base, 3)
    pair_dev = W_DEV // 2
    pair_total = WALKERS // 2
    heavy = jax.random.randint(first_key, (), 0, N_ROW)
    pair_ids = jnp.arange(pair_total, dtype=jnp.int32)
    is_heavy = pair_ids // pair_dev == heavy
    shuffled = jax.random.permutation(second_key, pair_total).astype(jnp.int32)
    scores = jnp.where(is_heavy, pair_total + shuffled, shuffled)
    ordering = jnp.argsort(scores, stable=True)
    ranked = jnp.zeros((pair_total,), jnp.int32).at[ordering].set(jnp.arange(pair_total, dtype=jnp.int32))
    others = (N_ROW - 1) * pair_dev
    fours = others // 4
    zero_end = 2 * fours + pair_dev
    pair_sum = jnp.where(ranked < fours, 4, jnp.where(ranked < zero_end, 0, 2))
    pair_sum = jnp.where(is_heavy, 4, pair_sum)
    split = jax.random.randint(third_key, (pair_total,), 0, 6)
    four_first = jnp.where(split % 3 == 0, 3, jnp.where(split % 3 == 1, 1, 2))
    two_first = jnp.where(split % 3 == 0, 1, jnp.where(split % 3 == 1, 2, 0))
    heavy_first = jnp.where(split % 2 == 0, 3, 1)
    first = jnp.where(pair_sum == 4, four_first, jnp.where(pair_sum == 2, two_first, 0))
    first = jnp.where(is_heavy, heavy_first, first)
    second = pair_sum - first
    return jnp.stack([first, second], axis=1).reshape(WALKERS).astype(jnp.int32)


def block_scale(stream_key, shape, pieces, least, high):
    gain = 1.0
    for axis_at, blocks in pieces:
        steps = jax.random.uniform(jax.random.fold_in(jax.random.fold_in(stream_key, 6), axis_at), (blocks,), jnp.float32, least / len(pieces), high / len(pieces))
        gain = gain * jnp.repeat(jnp.exp(steps), shape[axis_at] // blocks).reshape((-1,) + (1,) * (len(shape) - 1 - axis_at))
    return gain


def scatter_about(rng, dims, scale, most, pieces=(), held_as=jnp.bfloat16):
    drawn = scale * jax.random.normal(rng, dims, jnp.float32)
    if pieces:
        drawn = drawn * block_scale(rng, dims, pieces, -0.22, 0.18)
    return jnp.clip(drawn, -most, most).astype(held_as)


def setup_inputs(seed: int = 0, part: int = 0) -> dict:
    key_of = jax.random.split(jax.random.key(seed), 8)
    part_splits = jax.random.split(jax.random.fold_in(key_of[7], part), 8)
    walkers = scatter_about(part_splits[0], (WALKERS, ORBITALS, ELECTRONS), 1.0, 6.0, ((0, 16),))
    inv_intersection = scatter_about(part_splits[1], (WALKERS, ELECTRONS, ELECTRONS), ELECTRONS ** -0.5, 0.75, ((0, 16),))
    copies = draw_copies(jax.random.fold_in(jax.random.fold_in(key_of[7], part), 71), part)
    deal = jax.random.permutation(part_splits[3], N_ROW).astype(jnp.int32)
    trial = scatter_about(part_splits[4], (ORBITALS, ELECTRONS), 0.5, 6.0)
    chol = scatter_about(part_splits[5], (CHOL, ORBITALS, ORBITALS), (10.24 / (ORBITALS * CHOL) ** 0.5), 0.15625, ((1, 16),))
    noise = scatter_about(part_splits[6], (WALKERS, CHOL), 1.0, 6.0, ((0, 16),), jnp.float32)
    return dict(walkers=walkers, inv_intersection=inv_intersection, copies=copies, deal=deal, trial=trial, chol=chol, noise=noise)


root_step = 0.1


def reference(walkers, inv_intersection, copies, deal, trial, chol, noise):
    copy_ends = jnp.cumsum(copies).astype(jnp.int32)
    residue = jnp.argsort(deal).astype(jnp.int32)
    slot_ids = jnp.arange(WALKERS, dtype=jnp.int32)
    wanted = (slot_ids % W_DEV) * N_ROW + residue[slot_ids // W_DEV]
    parent = jnp.searchsorted(copy_ends, wanted, side="right").astype(jnp.int32)
    orbitals = walkers[parent]
    inverse = inv_intersection[parent]
    half_rotated = jnp.einsum("wmk,wkn->wmn", orbitals.astype(jnp.float32), inverse.astype(jnp.float32)).astype(jnp.bfloat16)
    density = jnp.einsum("win,kn->wik", half_rotated.astype(jnp.float32), trial.astype(jnp.float32)).astype(jnp.bfloat16)
    chol_flat = chol.reshape(CHOL, ORBITALS * ORBITALS)
    bias_raw = jnp.dot(density.reshape(WALKERS, ORBITALS * ORBITALS), chol_flat.T, preferred_element_type=jnp.float32)
    force_bias = root_step * bias_raw
    fields = (noise + jnp.clip(force_bias, -1.0, 1.0)).astype(jnp.bfloat16)
    propagator = jnp.dot(fields, chol_flat, preferred_element_type=jnp.float32).astype(jnp.bfloat16)
    propagator = propagator.reshape(WALKERS, ORBITALS, ORBITALS)
    current = orbitals
    summed = orbitals.astype(jnp.float32)
    for degree in range(1, 5):
        product = jnp.einsum("wik,wkn->win", propagator.astype(jnp.float32), current.astype(jnp.float32))
        current = (root_step / degree * product).astype(jnp.bfloat16)
        summed = summed + current.astype(jnp.float32)
    return summed.astype(jnp.bfloat16), force_bias
```

```python
import functools

import jax
import jax.numpy as jnp
from jax import lax
from jax.experimental import pallas as pl
from jax.experimental.pallas import tpu as pltpu
from jax.sharding import PartitionSpec as P

root_step = 0.1
MESH = pl.DeviceIdType.MESH
VM = pltpu.VMEM


def peer(q):
    me = lax.axis_index("row")
    other = me
    bit = 1
    while bit <= q:
        if q & bit:
            other = other + bit - 2 * bit * lax.rem(lax.div(me, bit), 2)
        bit *= 2
    return other


def greet(qs):
    barrier = pltpu.get_barrier_semaphore()
    for q in qs:
        pl.semaphore_signal(barrier, inc=1, device_id={"row": peer(q)}, device_id_type=MESH)
    pl.semaphore_wait(barrier, len(qs))


def density_kernel(pick_ref, theta_ref, trial_ref, out_ref):
    width, electrons = trial_ref.shape
    mine = jnp.dot(pick_ref[...], theta_ref[...], preferred_element_type=jnp.float32).astype(jnp.bfloat16)
    for row in range(theta_ref.shape[1] // electrons):
        out_ref[:, row * width : (row + 1) * width] = lax.dot_general(
            mine[:, row * electrons : (row + 1) * electrons],
            trial_ref[...],
            (((1,), (1,)), ((), ())),
            preferred_element_type=jnp.float32,
        ).astype(jnp.bfloat16)


def stages(bits):
    first = list(range(bits))
    second = [0] + list(range(2, bits)) + [1] if bits > 1 else first
    return first, second


def fields_kernel(n, part_ref, noise_ref, bias_ref, all_ref, got, held, total, send, recv):
    per, cols = noise_ref.shape
    half = cols // 2
    bits = n.bit_length() - 1
    orders = stages(bits)
    greet([1 << b for b in range(bits)])

    def lanes(h):
        return pl.ds(h * half, half)

    def rows(q):
        return pl.ds(q * per, per)

    live = [list(range(n)), list(range(n))]
    flying = [None, None]

    def launch(h, t):
        b = 1 << orders[h][t]
        copies = []
        for q in live[h]:
            if q & b:
                src = part_ref if t == 0 else held
                copy = pltpu.make_async_remote_copy(
                    src_ref=src.at[rows(q), lanes(h)],
                    dst_ref=got.at[rows(q), lanes(h)],
                    send_sem=send.at[h * n + q],
                    recv_sem=recv.at[h * n + q],
                    device_id={"row": peer(b)},
                    device_id_type=MESH,
                )
                copy.start()
                copies.append(copy)
        flying[h] = copies

    for h in range(2):
        launch(h, 0)
    for t in range(bits):
        for h in range(2):
            b = 1 << orders[h][t]
            for copy in flying[h]:
                copy.wait()
            live[h] = [q for q in live[h] if not q & b]
            src = part_ref if t == 0 else held
            for q in live[h]:
                value = src[rows(q), lanes(h)].astype(jnp.float32) + got[rows(q | b), lanes(h)].astype(jnp.float32)
                if t == bits - 1:
                    total[:, lanes(h)] = value
                else:
                    held[rows(q), lanes(h)] = value.astype(jnp.bfloat16)
            if t < bits - 1:
                launch(h, t + 1)

    have = [[0], [0]]

    def spread(h, t):
        b = 1 << orders[h][bits - 1 - t]
        copies = []
        for q in have[h]:
            copy = pltpu.make_async_remote_copy(
                src_ref=all_ref.at[rows(q), lanes(h)],
                dst_ref=all_ref.at[rows(q | b), lanes(h)],
                send_sem=send.at[(2 + h) * n + (q | b)],
                recv_sem=recv.at[(2 + h) * n + (q | b)],
                device_id={"row": peer(b)},
                device_id_type=MESH,
            )
            copy.start()
            copies.append(copy)
        have[h] = have[h] + [q | b for q in have[h]]
        flying[h] = copies

    for h in range(2):
        bias = root_step * total[:, lanes(h)]
        bias_ref[:, lanes(h)] = bias
        all_ref[rows(0), lanes(h)] = (noise_ref[:, lanes(h)] + jnp.clip(bias, -1.0, 1.0)).astype(jnp.bfloat16)
        spread(h, 0)
    for t in range(bits):
        for h in range(2):
            for copy in flying[h]:
                copy.wait()
            if t < bits - 1:
                spread(h, t + 1)


def deal_kernel(n, part_ref, out_ref, own_sem, send, recv):
    me = lax.axis_index("row")
    greet(list(range(1, n)))
    own = pltpu.make_async_copy(part_ref.at[0], out_ref.at[:, me], own_sem)
    own.start()
    copies = []
    for q in range(n - 1, 0, -1):
        copy = pltpu.make_async_remote_copy(
            src_ref=part_ref.at[q],
            dst_ref=out_ref.at[:, me],
            send_sem=send.at[q],
            recv_sem=recv.at[q],
            device_id={"row": peer(q)},
            device_id_type=MESH,
        )
        copy.start()
        copies.append(copy)
    for copy in copies:
        copy.wait()
    own.wait()


def local(walkers, inv_intersection, copies, deal, trial, chol, noise):
    n = lax.axis_size("row")
    me = lax.axis_index("row")
    per, orbitals_n, electrons = walkers.shape
    all_walkers = n * per
    g, own_rows, width = chol.shape
    chol_flat = chol.reshape(g, own_rows * width)

    theta = jnp.einsum("wmk,wkn->wmn", walkers, inv_intersection, preferred_element_type=jnp.float32)
    theta = theta.astype(jnp.bfloat16).reshape(per, n, own_rows * electrons).transpose(1, 0, 2)
    theta_rows = lax.all_to_all(theta, "row", split_axis=0, concat_axis=0, tiled=True)
    theta_rows = theta_rows.reshape(all_walkers, own_rows * electrons)

    everyone = lax.all_to_all(
        jnp.broadcast_to(copies[None], (n, per)), "row", split_axis=0, concat_axis=0, tiled=True
    ).reshape(all_walkers)
    old = jnp.arange(all_walkers, dtype=jnp.int32)
    copy_ends = jnp.sum(jnp.where(old[None, :] <= old[:, None], everyone[None, :], 0), axis=1)
    owners = jnp.arange(n, dtype=jnp.int32)
    residue = jnp.sum(jnp.where(deal[None, :] == owners[:, None], owners[None, :], 0), axis=1)
    slots = jnp.arange(per, dtype=jnp.int32)

    owner = jnp.bitwise_xor(owners, me)
    owner_residue = jnp.sum(jnp.where(deal[None, :] == owner[:, None], owners[None, :], 0), axis=1)
    wanted = (slots[None, :] * n + owner_residue[:, None]).reshape(all_walkers)
    parent = jnp.sum((copy_ends[None, :] <= wanted[:, None]).astype(jnp.int32), axis=1)
    pick = (parent[:, None] == old[None, :]).astype(jnp.bfloat16)

    capacity = (2 * per + n - 1) // n
    ends_by = copy_ends.reshape(n, per)
    starts_dev = ends_by[:, 0] - everyone.reshape(n, per)[:, 0]
    own_first = jnp.sum(jnp.where(owners == me, starts_dev, 0))
    own_count = jnp.sum(copies)
    own_ends = jnp.sum(jnp.where(slots[None, :] <= slots[:, None], copies[None, :], 0), axis=1)
    picks = jnp.arange(capacity, dtype=jnp.int32)[None, :]
    first_hit = own_first + jnp.mod(residue[:, None] - own_first, n)
    positions = (first_hit + picks * n).reshape(-1)
    usable = positions < own_first + own_count
    local_walker = jnp.sum((own_ends[None, :] <= (positions - own_first)[:, None]).astype(jnp.int32), axis=1)
    send_pick = ((local_walker[:, None] == slots[None, :]) & usable[:, None]).astype(jnp.bfloat16)
    flat = walkers.reshape(per, orbitals_n * electrons)
    sent = jnp.dot(send_pick, flat, preferred_element_type=jnp.float32).astype(jnp.bfloat16)
    got = lax.all_to_all(sent, "row", split_axis=0, concat_axis=0, tiled=True)
    own_parent = parent[:per]
    own_wanted = wanted[:per]
    source = own_parent // per
    source_first = jnp.sum(jnp.where(source[:, None] == owners[None, :], starts_dev[None, :], 0), axis=1)
    source_hit = source_first + jnp.mod(owner_residue[0] - source_first, n)
    received = source * capacity + (own_wanted - source_hit) // n
    take = (received[:, None] == jnp.arange(n * capacity)[None, :]).astype(jnp.bfloat16)
    orbitals = jnp.dot(take, got, preferred_element_type=jnp.float32).astype(jnp.bfloat16)
    orbitals = orbitals.reshape(per, orbitals_n, electrons)

    density = pl.pallas_call(
        density_kernel,
        out_shape=jax.ShapeDtypeStruct((all_walkers, own_rows * width), jnp.bfloat16),
        in_specs=[pl.BlockSpec(memory_space=VM)] * 3,
        out_specs=pl.BlockSpec(memory_space=VM),
        name="density",
    )(pick, theta_rows, trial)

    part = lax.dot_general(
        density, chol_flat, (((1,), (1,)), ((), ())), preferred_element_type=jnp.float32
    ).astype(jnp.bfloat16)
    force_bias, fields = pl.pallas_call(
        functools.partial(fields_kernel, n),
        out_shape=(
            jax.ShapeDtypeStruct((per, g), jnp.float32),
            jax.ShapeDtypeStruct((all_walkers, g), jnp.bfloat16),
        ),
        in_specs=[pl.BlockSpec(memory_space=VM)] * 2,
        out_specs=(pl.BlockSpec(memory_space=VM),) * 2,
        scratch_shapes=[
            pltpu.VMEM((all_walkers, g), jnp.bfloat16),
            pltpu.VMEM((all_walkers, g), jnp.bfloat16),
            pltpu.VMEM((per, g), jnp.float32),
            pltpu.SemaphoreType.DMA((4 * n,)),
            pltpu.SemaphoreType.DMA((4 * n,)),
        ],
        compiler_params=pltpu.CompilerParams(collective_id=0, has_side_effects=True),
        name="fields",
    )(part, noise)

    propagator_part = jnp.dot(fields, chol_flat, preferred_element_type=jnp.float32).astype(jnp.bfloat16)
    propagator_part = propagator_part.reshape(n, per, own_rows, width)
    propagator = pl.pallas_call(
        functools.partial(deal_kernel, n),
        out_shape=jax.ShapeDtypeStruct((per, n, own_rows, width), jnp.bfloat16),
        in_specs=[pl.BlockSpec(memory_space=VM)],
        out_specs=pl.BlockSpec(memory_space=VM),
        scratch_shapes=[
            pltpu.SemaphoreType.DMA,
            pltpu.SemaphoreType.DMA((n,)),
            pltpu.SemaphoreType.DMA((n,)),
        ],
        compiler_params=pltpu.CompilerParams(collective_id=1, has_side_effects=True),
        name="deal",
    )(propagator_part)
    propagator = propagator.reshape(per, n * own_rows, width)

    current = orbitals
    summed = orbitals.astype(jnp.float32)
    for degree in range(1, 5):
        product = jnp.einsum("wik,wkn->win", propagator, current, preferred_element_type=jnp.float32)
        current = (root_step / degree * product).astype(jnp.bfloat16)
        summed = summed + current.astype(jnp.float32)
    return (summed.astype(jnp.bfloat16), force_bias)


def solution(mesh):
    in_specs = (
        P(("groups", "row"), None, None),
        P(("groups", "row"), None, None),
        P(("groups", "row")),
        P("groups"),
        P("groups", None),
        P("groups", "row", None),
        P(("groups", "row"), None),
    )
    out_specs = (P(("groups", "row"), None, None), P(("groups", "row"), None))
    return jax.shard_map(local, mesh=mesh, in_specs=in_specs, out_specs=out_specs, check_vma=False)
```

```python
import functools

import jax
import jax.numpy as jnp
from jax import lax
from jax.experimental import pallas as pl
from jax.experimental.pallas import tpu as pltpu
from jax.sharding import PartitionSpec as P

root_step = 0.1
MESH = pl.DeviceIdType.MESH
VM = pltpu.VMEM


def peer(q):
    me = lax.axis_index("row")
    other = me
    bit = 1
    while bit <= q:
        if q & bit:
            other = other + bit - 2 * bit * lax.rem(lax.div(me, bit), 2)
        bit *= 2
    return other


def greet(qs):
    barrier = pltpu.get_barrier_semaphore()
    for q in qs:
        pl.semaphore_signal(barrier, inc=1, device_id={"row": peer(q)}, device_id_type=MESH)
    pl.semaphore_wait(barrier, len(qs))


def density_kernel(pick_ref, theta_ref, trial_ref, out_ref):
    width, electrons = trial_ref.shape
    mine = jnp.dot(pick_ref[...], theta_ref[...], preferred_element_type=jnp.float32).astype(jnp.bfloat16)
    for row in range(theta_ref.shape[1] // electrons):
        out_ref[:, row * width : (row + 1) * width] = lax.dot_general(
            mine[:, row * electrons : (row + 1) * electrons],
            trial_ref[...],
            (((1,), (1,)), ((), ())),
            preferred_element_type=jnp.float32,
        ).astype(jnp.bfloat16)


def order_of(bits, c):
    first = list(range(bits))
    second = [0] + list(range(2, bits)) + [1] if bits > 1 else first
    return second if c % 2 else first


def step_kernel(n, chunks, groups, density_ref, chol_hbm, noise_ref, bias_ref, out_ref,
                chol_ref, part, got, held, fields, total, product, load, send, recv, own_sem, deal_send, deal_recv):
    me = lax.axis_index("row")
    per, cols = noise_ref.shape
    wide = cols // chunks
    own_rows, _, width = product.shape
    tile = min(wide, 256)
    bits = n.bit_length() - 1

    def rows(q):
        return pl.ds(q * per, per)

    loads = []
    for c in range(chunks):
        copy = pltpu.make_async_copy(chol_hbm.at[pl.ds(c * wide, wide)], chol_ref.at[c], load.at[c])
        copy.start()
        loads.append(copy)
    greet(list(range(1, n)))

    live = [list(range(n)) for _ in range(chunks)]
    have = [[0] for _ in range(chunks)]
    flying = [None] * chunks

    def move(c, src, dst, pairs, b, base):
        copies = []
        for q, into in pairs:
            copy = pltpu.make_async_remote_copy(
                src_ref=src.at[c, rows(q)],
                dst_ref=dst.at[c, rows(into)],
                send_sem=send.at[base + c * n + into],
                recv_sem=recv.at[base + c * n + into],
                device_id={"row": peer(b)},
                device_id_type=MESH,
            )
            copy.start()
            copies.append(copy)
        flying[c] = copies

    def scatter(c, t):
        b = 1 << order_of(bits, c)[t]
        move(c, part if t == 0 else held, got, [(q, q) for q in live[c] if q & b], b, 0)

    def spread(c, t):
        b = 1 << order_of(bits, c)[bits - 1 - t]
        move(c, fields, fields, [(q, q | b) for q in have[c]], b, chunks * n)
        have[c] = have[c] + [q | b for q in have[c]]

    def land(c):
        for copy in flying[c]:
            copy.wait()

    def first_product(c):
        loads[c].wait()

        def body(i, carry):
            at = pl.ds(pl.multiple_of(i * tile, tile), tile)
            part[c, :, at] = lax.dot_general(
                density_ref[...], chol_ref[c, at, :], (((1,), (1,)), ((), ())), preferred_element_type=jnp.float32
            ).astype(jnp.bfloat16)
            return carry

        lax.fori_loop(0, wide // tile, body, 0)

    def second_product(c, low, high):
        def body(i, carry):
            at = pl.ds(pl.multiple_of(i * width, width), width)
            value = jnp.dot(fields[c], chol_ref[c, :, at], preferred_element_type=jnp.float32)
            if c > 0:
                value = value + total[i]
            if c < chunks - 1:
                total[i] = value
            else:
                product[i] = value.astype(jnp.bfloat16)
            return carry

        lax.fori_loop(low, high, body, 0)

    dealt = []

    def deal(s, low, high):
        own = pltpu.make_async_copy(
            product.at[low:high, rows(0)], out_ref.at[pl.ds(me * own_rows + low, high - low)], own_sem.at[s]
        )
        own.start()
        dealt.append(own)
        for q in range(n - 1, 0, -1):
            copy = pltpu.make_async_remote_copy(
                src_ref=product.at[low:high, rows(q)],
                dst_ref=out_ref.at[pl.ds(me * own_rows + low, high - low)],
                send_sem=deal_send.at[s * n + q],
                recv_sem=deal_recv.at[s * n + q],
                device_id={"row": peer(q)},
                device_id_type=MESH,
            )
            copy.start()
            dealt.append(copy)

    def stage(c, s):
        if s == 0:
            first_product(c)
            scatter(c, 0)
        elif s <= bits:
            t = s - 1
            b = 1 << order_of(bits, c)[t]
            land(c)
            live[c] = [q for q in live[c] if not q & b]
            src = part if t == 0 else held
            for q in live[c]:
                value = src[c, rows(q)].astype(jnp.float32) + got[c, rows(q | b)].astype(jnp.float32)
                if t < bits - 1:
                    held[c, rows(q)] = value.astype(jnp.bfloat16)
                else:
                    bias = root_step * value
                    at = pl.ds(c * wide, wide)
                    bias_ref[:, at] = bias
                    fields[c, rows(0)] = (noise_ref[:, at] + jnp.clip(bias, -1.0, 1.0)).astype(jnp.bfloat16)
            if t < bits - 1:
                scatter(c, t + 1)
            else:
                spread(c, 0)
        else:
            t = s - bits - 1
            land(c)
            if t < bits - 1:
                spread(c, t + 1)

    last = 2 * bits
    for tick in range(chunks + last):
        for c in range(chunks):
            if 0 <= tick - c <= last:
                stage(c, tick - c)
        done = tick - last
        if 0 <= done < chunks - 1:
            second_product(done, 0, own_rows)
    size = own_rows // groups
    for s in range(groups):
        second_product(chunks - 1, s * size, (s + 1) * size)
        deal(s, s * size, (s + 1) * size)
    for copy in dealt:
        copy.wait()


def local(walkers, inv_intersection, copies, deal, trial, chol, noise):
    n = lax.axis_size("row")
    me = lax.axis_index("row")
    per, orbitals_n, electrons = walkers.shape
    all_walkers = n * per
    g, own_rows, width = chol.shape
    chol_flat = chol.reshape(g, own_rows * width)

    theta = jnp.einsum("wmk,wkn->wmn", walkers, inv_intersection, preferred_element_type=jnp.float32)
    theta = theta.astype(jnp.bfloat16).reshape(per, n, own_rows * electrons).transpose(1, 0, 2)
    theta_rows = lax.all_to_all(theta, "row", split_axis=0, concat_axis=0, tiled=True)
    theta_rows = theta_rows.reshape(all_walkers, own_rows * electrons)

    everyone = lax.all_to_all(
        jnp.broadcast_to(copies[None], (n, per)), "row", split_axis=0, concat_axis=0, tiled=True
    ).reshape(all_walkers)
    old = jnp.arange(all_walkers, dtype=jnp.int32)
    copy_ends = jnp.sum(jnp.where(old[None, :] <= old[:, None], everyone[None, :], 0), axis=1)
    owners = jnp.arange(n, dtype=jnp.int32)
    residue = jnp.sum(jnp.where(deal[None, :] == owners[:, None], owners[None, :], 0), axis=1)
    slots = jnp.arange(per, dtype=jnp.int32)

    owner = jnp.bitwise_xor(owners, me)
    owner_residue = jnp.sum(jnp.where(deal[None, :] == owner[:, None], owners[None, :], 0), axis=1)
    wanted = (slots[None, :] * n + owner_residue[:, None]).reshape(all_walkers)
    parent = jnp.sum((copy_ends[None, :] <= wanted[:, None]).astype(jnp.int32), axis=1)
    pick = (parent[:, None] == old[None, :]).astype(jnp.bfloat16)

    capacity = (2 * per + n - 1) // n
    ends_by = copy_ends.reshape(n, per)
    starts_dev = ends_by[:, 0] - everyone.reshape(n, per)[:, 0]
    own_first = jnp.sum(jnp.where(owners == me, starts_dev, 0))
    own_count = jnp.sum(copies)
    own_ends = jnp.sum(jnp.where(slots[None, :] <= slots[:, None], copies[None, :], 0), axis=1)
    picks = jnp.arange(capacity, dtype=jnp.int32)[None, :]
    first_hit = own_first + jnp.mod(residue[:, None] - own_first, n)
    positions = (first_hit + picks * n).reshape(-1)
    usable = positions < own_first + own_count
    local_walker = jnp.sum((own_ends[None, :] <= (positions - own_first)[:, None]).astype(jnp.int32), axis=1)
    send_pick = ((local_walker[:, None] == slots[None, :]) & usable[:, None]).astype(jnp.bfloat16)
    flat = walkers.reshape(per, orbitals_n * electrons)
    sent = jnp.dot(send_pick, flat, preferred_element_type=jnp.float32).astype(jnp.bfloat16)
    got = lax.all_to_all(sent, "row", split_axis=0, concat_axis=0, tiled=True)
    own_parent = parent[:per]
    own_wanted = wanted[:per]
    source = own_parent // per
    source_first = jnp.sum(jnp.where(source[:, None] == owners[None, :], starts_dev[None, :], 0), axis=1)
    source_hit = source_first + jnp.mod(owner_residue[0] - source_first, n)
    received = source * capacity + (own_wanted - source_hit) // n
    take = (received[:, None] == jnp.arange(n * capacity)[None, :]).astype(jnp.bfloat16)
    orbitals = jnp.dot(take, got, preferred_element_type=jnp.float32).astype(jnp.bfloat16)
    orbitals = orbitals.reshape(per, orbitals_n, electrons)

    density = pl.pallas_call(
        density_kernel,
        out_shape=jax.ShapeDtypeStruct((all_walkers, own_rows * width), jnp.bfloat16),
        in_specs=[pl.BlockSpec(memory_space=VM)] * 3,
        out_specs=pl.BlockSpec(memory_space=VM),
        name="density",
    )(pick, theta_rows, trial)

    chunks, groups = 4, 4
    wide = g // chunks
    force_bias, dealt = pl.pallas_call(
        functools.partial(step_kernel, n, chunks, groups),
        out_shape=(
            jax.ShapeDtypeStruct((per, g), jnp.float32),
            jax.ShapeDtypeStruct((n * own_rows, per, width), jnp.bfloat16),
        ),
        in_specs=[
            pl.BlockSpec(memory_space=VM),
            pl.BlockSpec(memory_space=pl.ANY),
            pl.BlockSpec(memory_space=VM),
        ],
        out_specs=(pl.BlockSpec(memory_space=VM),) * 2,
        scratch_shapes=[
            pltpu.VMEM((chunks, wide, own_rows * width), jnp.bfloat16),
            pltpu.VMEM((chunks, all_walkers, wide), jnp.bfloat16),
            pltpu.VMEM((chunks, all_walkers, wide), jnp.bfloat16),
            pltpu.VMEM((chunks, all_walkers, wide), jnp.bfloat16),
            pltpu.VMEM((chunks, all_walkers, wide), jnp.bfloat16),
            pltpu.VMEM((own_rows, all_walkers, width), jnp.float32),
            pltpu.VMEM((own_rows, all_walkers, width), jnp.bfloat16),
            pltpu.SemaphoreType.DMA((chunks,)),
            pltpu.SemaphoreType.DMA((2 * chunks * n,)),
            pltpu.SemaphoreType.DMA((2 * chunks * n,)),
            pltpu.SemaphoreType.DMA((groups,)),
            pltpu.SemaphoreType.DMA((groups * n,)),
            pltpu.SemaphoreType.DMA((groups * n,)),
        ],
        compiler_params=pltpu.CompilerParams(
            collective_id=0, has_side_effects=True, vmem_limit_bytes=62 * 2**20
        ),
        name="step",
    )(density, chol_flat, noise)
    propagator = dealt.transpose(1, 0, 2)

    current = orbitals
    summed = orbitals.astype(jnp.float32)
    for degree in range(1, 5):
        product = jnp.einsum("wik,wkn->win", propagator, current, preferred_element_type=jnp.float32)
        current = (root_step / degree * product).astype(jnp.bfloat16)
        summed = summed + current.astype(jnp.float32)
    return (summed.astype(jnp.bfloat16), force_bias)


def solution(mesh):
    in_specs = (
        P(("groups", "row"), None, None),
        P(("groups", "row"), None, None),
        P(("groups", "row")),
        P("groups"),
        P("groups", None),
        P("groups", "row", None),
        P(("groups", "row"), None),
    )
    out_specs = (P(("groups", "row"), None, None), P(("groups", "row"), None))
    return jax.shard_map(local, mesh=mesh, in_specs=in_specs, out_specs=out_specs, check_vma=False)
```

```python
import functools

import jax
import jax.numpy as jnp
from jax import lax
from jax.experimental import pallas as pl
from jax.experimental.pallas import tpu as pltpu
from jax.sharding import PartitionSpec as P

root_step = 0.1
MESH = pl.DeviceIdType.MESH
VM = pltpu.VMEM


def peer(q):
    me = lax.axis_index("row")
    other = me
    bit = 1
    while bit <= q:
        if q & bit:
            other = other + bit - 2 * bit * lax.rem(lax.div(me, bit), 2)
        bit *= 2
    return other


def greet(qs):
    barrier = pltpu.get_barrier_semaphore()
    for q in qs:
        pl.semaphore_signal(barrier, inc=1, device_id={"row": peer(q)}, device_id_type=MESH)
    pl.semaphore_wait(barrier, len(qs))


def density_kernel(n, per, capacity, theta_ref, deal_ref, trial_ref, chol_hbm, out_ref, sent_ref, take_ref):
    me = lax.axis_index("row")
    width, electrons = trial_ref.shape
    walkers = n * per
    used = theta_ref.shape[1] - 128
    own_bits = per.bit_length() - 1
    cap_bits = capacity.bit_length() - 1
    slots = n * capacity

    def down(length):
        return lax.broadcasted_iota(jnp.int32, (length, 1), 0)

    def along(length):
        return lax.broadcasted_iota(jnp.int32, (1, length), 1)

    count = theta_ref[:, used : used + 1].astype(jnp.float32)

    def counted(mask):
        return jnp.sum(jnp.where(mask, count, 0.0), axis=0, keepdims=True).astype(jnp.int32)

    deal = deal_ref[...]

    def residue(owner):
        return jnp.sum(
            jnp.where(deal == owner, along(n), 0).astype(jnp.float32), axis=1, keepdims=True
        ).astype(jnp.int32)

    ends = counted(down(walkers) <= along(walkers))
    starts = counted(down(walkers) < along(walkers))

    def holds(position):
        return jnp.where((starts <= position) & (position < ends), 1.0, 0.0).astype(jnp.bfloat16)

    new = down(walkers)
    wanted = jnp.bitwise_and(new, per - 1) * n + residue(jnp.bitwise_xor(jnp.right_shift(new, own_bits), me))
    mine = jnp.dot(holds(wanted), theta_ref[:, :used], preferred_element_type=jnp.float32).astype(jnp.bfloat16)
    for row in range(used // electrons):
        out_ref[:, row * width : (row + 1) * width] = lax.dot_general(
            mine[:, row * electrons : (row + 1) * electrons],
            trial_ref[...],
            (((1,), (1,)), ((), ())),
            preferred_element_type=jnp.float32,
        ).astype(jnp.bfloat16)

    line = down(slots)
    own_first = counted(down(walkers) < me * per)
    to = residue(jnp.right_shift(line, cap_bits))
    step = jnp.bitwise_and(line, capacity - 1) * n
    sent_ref[...] = holds(own_first + jnp.bitwise_and(to - own_first + walkers, n - 1) + step)

    line = along(slots)
    source = jnp.right_shift(line, cap_bits)
    first = counted(down(walkers) < source * per)
    past = counted(down(walkers) < (source + 1) * per)
    own_residue = residue(jnp.zeros((1, 1), jnp.int32) + me)
    place = first + jnp.bitwise_and(own_residue - first + walkers, n - 1) + jnp.bitwise_and(line, capacity - 1) * n
    own_wanted = down(per) * n + own_residue
    take_ref[...] = jnp.where((place == own_wanted) & (place < past), 1.0, 0.0).astype(jnp.bfloat16)


def order_of(bits, c):
    first = list(range(bits))
    second = [0] + list(range(2, bits)) + [1] if bits > 1 else first
    return second if c % 2 else first


def step_kernel(n, chunks, groups, density_ref, chol_hbm, noise_ref, bias_ref, out_ref,
                chol_ref, part, got, held, fields, total, product, load, send, recv, own_sem, deal_send, deal_recv):
    me = lax.axis_index("row")
    per, cols = noise_ref.shape
    wide = cols // chunks
    own_rows, _, width = product.shape
    tile = min(wide, 256)
    bits = n.bit_length() - 1

    def rows(q):
        return pl.ds(q * per, per)

    loads = []
    for c in range(chunks):
        copy = pltpu.make_async_copy(chol_hbm.at[pl.ds(c * wide, wide)], chol_ref.at[c], load.at[c])
        copy.start()
        loads.append(copy)
    greet(list(range(1, n)))

    live = [list(range(n)) for _ in range(chunks)]
    have = [[0] for _ in range(chunks)]
    flying = [None] * chunks

    def move(c, src, dst, pairs, b, base):
        copies = []
        for q, into in pairs:
            copy = pltpu.make_async_remote_copy(
                src_ref=src.at[c, rows(q)],
                dst_ref=dst.at[c, rows(into)],
                send_sem=send.at[base + c * n + into],
                recv_sem=recv.at[base + c * n + into],
                device_id={"row": peer(b)},
                device_id_type=MESH,
            )
            copy.start()
            copies.append(copy)
        flying[c] = copies

    def scatter(c, t):
        b = 1 << order_of(bits, c)[t]
        move(c, part if t == 0 else held, got, [(q, q) for q in live[c] if q & b], b, 0)

    def spread(c, t):
        b = 1 << order_of(bits, c)[bits - 1 - t]
        move(c, fields, fields, [(q, q | b) for q in have[c]], b, chunks * n)
        have[c] = have[c] + [q | b for q in have[c]]

    def land(c):
        for copy in flying[c]:
            copy.wait()

    def first_product(c):
        loads[c].wait()

        def body(i, carry):
            at = pl.ds(pl.multiple_of(i * tile, tile), tile)
            part[c, :, at] = lax.dot_general(
                density_ref[...], chol_ref[c, at, :], (((1,), (1,)), ((), ())), preferred_element_type=jnp.float32
            ).astype(jnp.bfloat16)
            return carry

        lax.fori_loop(0, wide // tile, body, 0)

    def second_product(c, low, high):
        def body(i, carry):
            at = pl.ds(pl.multiple_of(i * width, width), width)
            value = jnp.dot(fields[c], chol_ref[c, :, at], preferred_element_type=jnp.float32)
            if c > 0:
                value = value + total[i]
            if c < chunks - 1:
                total[i] = value
            else:
                product[i] = value.astype(jnp.bfloat16)
            return carry

        lax.fori_loop(low, high, body, 0)

    dealt = []

    def deal(s, low, high):
        own = pltpu.make_async_copy(
            product.at[low:high, rows(0)], out_ref.at[pl.ds(me * own_rows + low, high - low)], own_sem.at[s]
        )
        own.start()
        dealt.append(own)
        for q in range(n - 1, 0, -1):
            copy = pltpu.make_async_remote_copy(
                src_ref=product.at[low:high, rows(q)],
                dst_ref=out_ref.at[pl.ds(me * own_rows + low, high - low)],
                send_sem=deal_send.at[s * n + q],
                recv_sem=deal_recv.at[s * n + q],
                device_id={"row": peer(q)},
                device_id_type=MESH,
            )
            copy.start()
            dealt.append(copy)

    def stage(c, s):
        if s == 0:
            first_product(c)
            scatter(c, 0)
        elif s <= bits:
            t = s - 1
            b = 1 << order_of(bits, c)[t]
            land(c)
            live[c] = [q for q in live[c] if not q & b]
            src = part if t == 0 else held
            for q in live[c]:
                value = src[c, rows(q)].astype(jnp.float32) + got[c, rows(q | b)].astype(jnp.float32)
                if t < bits - 1:
                    held[c, rows(q)] = value.astype(jnp.bfloat16)
                else:
                    bias = root_step * value
                    at = pl.ds(c * wide, wide)
                    bias_ref[:, at] = bias
                    fields[c, rows(0)] = (noise_ref[:, at] + jnp.clip(bias, -1.0, 1.0)).astype(jnp.bfloat16)
            if t < bits - 1:
                scatter(c, t + 1)
            else:
                spread(c, 0)
        else:
            t = s - bits - 1
            land(c)
            if t < bits - 1:
                spread(c, t + 1)

    last = 2 * bits
    for tick in range(chunks + last):
        for c in range(chunks):
            if 0 <= tick - c <= last:
                stage(c, tick - c)
        done = tick - last
        if 0 <= done < chunks - 1:
            second_product(done, 0, own_rows)
    size = own_rows // groups
    for s in range(groups):
        second_product(chunks - 1, s * size, (s + 1) * size)
        deal(s, s * size, (s + 1) * size)
    for copy in dealt:
        copy.wait()


def local(walkers, inv_intersection, copies, deal, trial, chol, noise):
    n = lax.axis_size("row")
    me = lax.axis_index("row")
    per, orbitals_n, electrons = walkers.shape
    all_walkers = n * per
    g, own_rows, width = chol.shape
    chol_flat = chol.reshape(g, own_rows * width)

    theta = jnp.einsum("wmk,wkn->wmn", walkers, inv_intersection, preferred_element_type=jnp.float32)
    theta = theta.astype(jnp.bfloat16).reshape(per, n, own_rows * electrons).transpose(1, 0, 2)
    counts = jnp.broadcast_to(copies.astype(jnp.bfloat16)[None, :, None], (n, per, 128))
    theta = jnp.concatenate([theta, counts], axis=2)
    theta_rows = lax.all_to_all(theta, "row", split_axis=0, concat_axis=0, tiled=True)
    theta_rows = theta_rows.reshape(all_walkers, own_rows * electrons + 128)

    capacity = (2 * per + n - 1) // n
    density, sent_all, take = pl.pallas_call(
        functools.partial(density_kernel, n, per, capacity),
        out_shape=(
            jax.ShapeDtypeStruct((all_walkers, own_rows * width), jnp.bfloat16),
            jax.ShapeDtypeStruct((n * capacity, all_walkers), jnp.bfloat16),
            jax.ShapeDtypeStruct((per, n * capacity), jnp.bfloat16),
        ),
        in_specs=[pl.BlockSpec(memory_space=VM)] * 3 + [pl.BlockSpec(memory_space=pl.ANY)],
        out_specs=(pl.BlockSpec(memory_space=VM),) * 3,
        name="density",
    )(theta_rows, deal.reshape(1, n), trial, chol_flat)

    flat = walkers.reshape(per, orbitals_n * electrons)
    send_pick = lax.dynamic_slice(sent_all, (0, me * per), (n * capacity, per))
    sent = jnp.dot(send_pick, flat, preferred_element_type=jnp.float32).astype(jnp.bfloat16)
    got = lax.all_to_all(sent, "row", split_axis=0, concat_axis=0, tiled=True)
    orbitals = jnp.dot(take, got, preferred_element_type=jnp.float32).astype(jnp.bfloat16)
    orbitals = orbitals.reshape(per, orbitals_n, electrons)

    chunks, groups = 4, 4
    wide = g // chunks
    force_bias, dealt = pl.pallas_call(
        functools.partial(step_kernel, n, chunks, groups),
        out_shape=(
            jax.ShapeDtypeStruct((per, g), jnp.float32),
            jax.ShapeDtypeStruct((n * own_rows, per, width), jnp.bfloat16),
        ),
        in_specs=[
            pl.BlockSpec(memory_space=VM),
            pl.BlockSpec(memory_space=pl.ANY),
            pl.BlockSpec(memory_space=VM),
        ],
        out_specs=(pl.BlockSpec(memory_space=VM),) * 2,
        scratch_shapes=[
            pltpu.VMEM((chunks, wide, own_rows * width), jnp.bfloat16),
            pltpu.VMEM((chunks, all_walkers, wide), jnp.bfloat16),
            pltpu.VMEM((chunks, all_walkers, wide), jnp.bfloat16),
            pltpu.VMEM((chunks, all_walkers, wide), jnp.bfloat16),
            pltpu.VMEM((chunks, all_walkers, wide), jnp.bfloat16),
            pltpu.VMEM((own_rows, all_walkers, width), jnp.float32),
            pltpu.VMEM((own_rows, all_walkers, width), jnp.bfloat16),
            pltpu.SemaphoreType.DMA((chunks,)),
            pltpu.SemaphoreType.DMA((2 * chunks * n,)),
            pltpu.SemaphoreType.DMA((2 * chunks * n,)),
            pltpu.SemaphoreType.DMA((groups,)),
            pltpu.SemaphoreType.DMA((groups * n,)),
            pltpu.SemaphoreType.DMA((groups * n,)),
        ],
        compiler_params=pltpu.CompilerParams(
            collective_id=0, has_side_effects=True, vmem_limit_bytes=62 * 2**20
        ),
        name="step",
    )(density, chol_flat, noise)
    propagator = dealt.transpose(1, 0, 2)

    current = orbitals
    summed = orbitals.astype(jnp.float32)
    for degree in range(1, 5):
        product = jnp.einsum("wik,wkn->win", propagator, current, preferred_element_type=jnp.float32)
        current = (root_step / degree * product).astype(jnp.bfloat16)
        summed = summed + current.astype(jnp.float32)
    return (summed.astype(jnp.bfloat16), force_bias)


def solution(mesh):
    in_specs = (
        P(("groups", "row"), None, None),
        P(("groups", "row"), None, None),
        P(("groups", "row")),
        P("groups"),
        P("groups", None),
        P("groups", "row", None),
        P(("groups", "row"), None),
    )
    out_specs = (P(("groups", "row"), None, None), P(("groups", "row"), None))
    return jax.shard_map(local, mesh=mesh, in_specs=in_specs, out_specs=out_specs, check_vma=False)
```

```python
import functools

import jax
import jax.numpy as jnp
from jax import lax
from jax.experimental import pallas as pl
from jax.experimental.pallas import tpu as pltpu
from jax.sharding import PartitionSpec as P

root_step = 0.1
MESH = pl.DeviceIdType.MESH
VM = pltpu.VMEM


def peer(q):
    me = lax.axis_index("row")
    other = me
    bit = 1
    while bit <= q:
        if q & bit:
            other = other + bit - 2 * bit * lax.rem(lax.div(me, bit), 2)
        bit *= 2
    return other


def greet(qs):
    barrier = pltpu.get_barrier_semaphore()
    for q in qs:
        pl.semaphore_signal(barrier, inc=1, device_id={"row": peer(q)}, device_id_type=MESH)
    pl.semaphore_wait(barrier, len(qs))


def density_kernel(n, per, capacity, theta_ref, deal_ref, trial_ref, chol_hbm, out_ref, sent_ref, take_ref):
    me = lax.axis_index("row")
    width, electrons = trial_ref.shape
    walkers = n * per
    used = theta_ref.shape[1] - 128
    own_bits = per.bit_length() - 1
    cap_bits = capacity.bit_length() - 1
    slots = n * capacity

    def down(length):
        return lax.broadcasted_iota(jnp.int32, (length, 1), 0)

    def along(length):
        return lax.broadcasted_iota(jnp.int32, (1, length), 1)

    count = theta_ref[:, used : used + 1].astype(jnp.float32)

    def counted(mask):
        return jnp.sum(jnp.where(mask, count, 0.0), axis=0, keepdims=True).astype(jnp.int32)

    deal = deal_ref[...]

    def residue(owner):
        return jnp.sum(
            jnp.where(deal == owner, along(n), 0).astype(jnp.float32), axis=1, keepdims=True
        ).astype(jnp.int32)

    ends = counted(down(walkers) <= along(walkers))
    starts = counted(down(walkers) < along(walkers))

    def holds(position):
        return jnp.where((starts <= position) & (position < ends), 1.0, 0.0).astype(jnp.bfloat16)

    new = down(walkers)
    wanted = jnp.bitwise_and(new, per - 1) * n + residue(jnp.bitwise_xor(jnp.right_shift(new, own_bits), me))
    mine = jnp.dot(holds(wanted), theta_ref[:, :used], preferred_element_type=jnp.float32).astype(jnp.bfloat16)
    for row in range(used // electrons):
        out_ref[:, row * width : (row + 1) * width] = lax.dot_general(
            mine[:, row * electrons : (row + 1) * electrons],
            trial_ref[...],
            (((1,), (1,)), ((), ())),
            preferred_element_type=jnp.float32,
        ).astype(jnp.bfloat16)

    line = down(slots)
    own_first = counted(down(walkers) < me * per)
    to = residue(jnp.right_shift(line, cap_bits))
    step = jnp.bitwise_and(line, capacity - 1) * n
    sent_ref[...] = holds(own_first + jnp.bitwise_and(to - own_first + walkers, n - 1) + step)

    line = along(slots)
    source = jnp.right_shift(line, cap_bits)
    first = counted(down(walkers) < source * per)
    past = counted(down(walkers) < (source + 1) * per)
    own_residue = residue(jnp.zeros((1, 1), jnp.int32) + me)
    place = first + jnp.bitwise_and(own_residue - first + walkers, n - 1) + jnp.bitwise_and(line, capacity - 1) * n
    own_wanted = down(per) * n + own_residue
    take_ref[...] = jnp.where((place == own_wanted) & (place < past), 1.0, 0.0).astype(jnp.bfloat16)


def order_of(bits, c):
    first = list(range(bits))
    second = [0] + list(range(2, bits)) + [1] if bits > 1 else first
    return second if c % 2 else first


def step_kernel(n, chunks, groups, density_ref, chol_hbm, noise_ref, bias_ref, out_ref,
                chol_ref, part, got, held, fields, total, product, load, send, recv, own_sem, deal_send, deal_recv):
    me = lax.axis_index("row")
    per, cols = noise_ref.shape
    wide = cols // chunks
    own_rows, _, width = product.shape
    tile = min(wide, 256)
    bits = n.bit_length() - 1

    def rows(q):
        return pl.ds(q * per, per)

    loads = []
    for c in range(chunks):
        copy = pltpu.make_async_copy(chol_hbm.at[pl.ds(c * wide, wide)], chol_ref.at[c], load.at[c])
        copy.start()
        loads.append(copy)
    greet(list(range(1, n)))

    live = [list(range(n)) for _ in range(chunks)]
    have = [[0] for _ in range(chunks)]
    flying = [None] * chunks

    def move(c, src, dst, pairs, b, base):
        copies = []
        for q, into in pairs:
            copy = pltpu.make_async_remote_copy(
                src_ref=src.at[c, rows(q)],
                dst_ref=dst.at[c, rows(into)],
                send_sem=send.at[base + c * n + into],
                recv_sem=recv.at[base + c * n + into],
                device_id={"row": peer(b)},
                device_id_type=MESH,
            )
            copy.start()
            copies.append(copy)
        flying[c] = copies

    def scatter(c, t):
        b = 1 << order_of(bits, c)[t]
        move(c, part if t == 0 else held, got, [(q, q) for q in live[c] if q & b], b, 0)

    def spread(c, t):
        b = 1 << order_of(bits, c)[bits - 1 - t]
        move(c, fields, fields, [(q, q | b) for q in have[c]], b, chunks * n)
        have[c] = have[c] + [q | b for q in have[c]]

    def land(c):
        for copy in flying[c]:
            copy.wait()

    def first_product(c):
        loads[c].wait()

        def body(i, carry):
            at = pl.ds(pl.multiple_of(i * tile, tile), tile)
            part[c, :, at] = lax.dot_general(
                density_ref[...], chol_ref[c, at, :], (((1,), (1,)), ((), ())), preferred_element_type=jnp.float32
            ).astype(jnp.bfloat16)
            return carry

        lax.fori_loop(0, wide // tile, body, 0)

    def second_product(c, low, high):
        def body(i, carry):
            at = pl.ds(pl.multiple_of(i * width, width), width)
            value = jnp.dot(fields[c], chol_ref[c, :, at], preferred_element_type=jnp.float32)
            if c > 0:
                value = value + total[i]
            if c < chunks - 1:
                total[i] = value
            else:
                product[i] = value.astype(jnp.bfloat16)
            return carry

        lax.fori_loop(low, high, body, 0)

    dealt = []

    def deal(s, low, high):
        own = pltpu.make_async_copy(
            product.at[low:high, rows(0)], out_ref.at[pl.ds(me * own_rows + low, high - low)], own_sem.at[s]
        )
        own.start()
        dealt.append(own)
        for q in range(n - 1, 0, -1):
            copy = pltpu.make_async_remote_copy(
                src_ref=product.at[low:high, rows(q)],
                dst_ref=out_ref.at[pl.ds(me * own_rows + low, high - low)],
                send_sem=deal_send.at[s * n + q],
                recv_sem=deal_recv.at[s * n + q],
                device_id={"row": peer(q)},
                device_id_type=MESH,
            )
            copy.start()
            dealt.append(copy)

    def stage(c, s):
        if s == 0:
            first_product(c)
            scatter(c, 0)
        elif s <= bits:
            t = s - 1
            b = 1 << order_of(bits, c)[t]
            land(c)
            live[c] = [q for q in live[c] if not q & b]
            src = part if t == 0 else held
            for q in live[c]:
                value = src[c, rows(q)].astype(jnp.float32) + got[c, rows(q | b)].astype(jnp.float32)
                if t < bits - 1:
                    held[c, rows(q)] = value.astype(jnp.bfloat16)
                else:
                    bias = root_step * value
                    at = pl.ds(c * wide, wide)
                    bias_ref[:, at] = bias
                    fields[c, rows(0)] = (noise_ref[:, at] + jnp.clip(bias, -1.0, 1.0)).astype(jnp.bfloat16)
            if t < bits - 1:
                scatter(c, t + 1)
            else:
                spread(c, 0)
        else:
            t = s - bits - 1
            land(c)
            if t < bits - 1:
                spread(c, t + 1)

    last = 2 * bits
    for tick in range(chunks + last):
        for c in range(chunks):
            if 0 <= tick - c <= last:
                stage(c, tick - c)
        done = tick - last
        if 0 <= done < chunks - 1:
            second_product(done, 0, own_rows)
    size = own_rows // groups
    for s in range(groups):
        second_product(chunks - 1, s * size, (s + 1) * size)
        deal(s, s * size, (s + 1) * size)
    for copy in dealt:
        copy.wait()


def local(walkers, inv_intersection, copies, deal, trial, chol, noise):
    n = lax.axis_size("row")
    me = lax.axis_index("row")
    per, orbitals_n, electrons = walkers.shape
    all_walkers = n * per
    g, own_rows, width = chol.shape
    chol_flat = chol.reshape(g, own_rows * width)

    theta = jnp.einsum("wmk,wkn->wmn", walkers, inv_intersection, preferred_element_type=jnp.float32)
    theta = theta.astype(jnp.bfloat16).reshape(per, n, own_rows * electrons).transpose(1, 0, 2)
    counts = jnp.broadcast_to(copies.astype(jnp.bfloat16)[None, :, None], (n, per, 128))
    theta = jnp.concatenate([theta, counts], axis=2)
    theta_rows = lax.all_to_all(theta, "row", split_axis=0, concat_axis=0, tiled=True)
    theta_rows = theta_rows.reshape(all_walkers, own_rows * electrons + 128)

    capacity = (2 * per + n - 1) // n
    density, sent_all, take = pl.pallas_call(
        functools.partial(density_kernel, n, per, capacity),
        out_shape=(
            jax.ShapeDtypeStruct((all_walkers, own_rows * width), jnp.bfloat16),
            jax.ShapeDtypeStruct((n * capacity, all_walkers), jnp.bfloat16),
            jax.ShapeDtypeStruct((per, n * capacity), jnp.bfloat16),
        ),
        in_specs=[pl.BlockSpec(memory_space=VM)] * 3 + [pl.BlockSpec(memory_space=pl.ANY)],
        out_specs=(pl.BlockSpec(memory_space=VM),) * 3,
        name="density",
    )(theta_rows, deal.reshape(1, n), trial, chol_flat)

    flat = walkers.reshape(per, orbitals_n * electrons)
    send_pick = lax.dynamic_slice(sent_all, (0, me * per), (n * capacity, per))
    sent = jnp.dot(send_pick, flat, preferred_element_type=jnp.float32).astype(jnp.bfloat16)
    got = lax.all_to_all(sent, "row", split_axis=0, concat_axis=0, tiled=True)
    orbitals = jnp.dot(take, got, preferred_element_type=jnp.float32).astype(jnp.bfloat16)
    orbitals = orbitals.reshape(per, orbitals_n, electrons)

    chunks, groups = 8, 4
    wide = g // chunks
    force_bias, dealt = pl.pallas_call(
        functools.partial(step_kernel, n, chunks, groups),
        out_shape=(
            jax.ShapeDtypeStruct((per, g), jnp.float32),
            jax.ShapeDtypeStruct((n * own_rows, per, width), jnp.bfloat16),
        ),
        in_specs=[
            pl.BlockSpec(memory_space=VM),
            pl.BlockSpec(memory_space=pl.ANY),
            pl.BlockSpec(memory_space=VM),
        ],
        out_specs=(pl.BlockSpec(memory_space=VM),) * 2,
        scratch_shapes=[
            pltpu.VMEM((chunks, wide, own_rows * width), jnp.bfloat16),
            pltpu.VMEM((chunks, all_walkers, wide), jnp.bfloat16),
            pltpu.VMEM((chunks, all_walkers, wide), jnp.bfloat16),
            pltpu.VMEM((chunks, all_walkers, wide), jnp.bfloat16),
            pltpu.VMEM((chunks, all_walkers, wide), jnp.bfloat16),
            pltpu.VMEM((own_rows, all_walkers, width), jnp.float32),
            pltpu.VMEM((own_rows, all_walkers, width), jnp.bfloat16),
            pltpu.SemaphoreType.DMA((chunks,)),
            pltpu.SemaphoreType.DMA((2 * chunks * n,)),
            pltpu.SemaphoreType.DMA((2 * chunks * n,)),
            pltpu.SemaphoreType.DMA((groups,)),
            pltpu.SemaphoreType.DMA((groups * n,)),
            pltpu.SemaphoreType.DMA((groups * n,)),
        ],
        compiler_params=pltpu.CompilerParams(
            collective_id=0, has_side_effects=True, vmem_limit_bytes=62 * 2**20
        ),
        name="step",
    )(density, chol_flat, noise)
    propagator = dealt.transpose(1, 0, 2)

    current = orbitals
    summed = orbitals.astype(jnp.float32)
    for degree in range(1, 5):
        product = jnp.einsum("wik,wkn->win", propagator, current, preferred_element_type=jnp.float32)
        current = (root_step / degree * product).astype(jnp.bfloat16)
        summed = summed + current.astype(jnp.float32)
    return (summed.astype(jnp.bfloat16), force_bias)


def solution(mesh):
    in_specs = (
        P(("groups", "row"), None, None),
        P(("groups", "row"), None, None),
        P(("groups", "row")),
        P("groups"),
        P("groups", None),
        P("groups", "row", None),
        P(("groups", "row"), None),
    )
    out_specs = (P(("groups", "row"), None, None), P(("groups", "row"), None))
    return jax.shard_map(local, mesh=mesh, in_specs=in_specs, out_specs=out_specs, check_vma=False)
```
